512 devices in a mesh: tm: 16 (over z), height: 8 (over x, y_lo), width: 4 (over y_hi, core).
Axes of the slice: x: 4, y: 4 (y_hi: 2, y_lo: 2; y = y_hi * 2 + y_lo), z: 16, core: 2. Of those that a mesh axis runs over, the one named last changes fastest.
Arguments:
- video_in: bfloat16 [64, 64, 6144], P('tm', 'height', 'width'), may hold values from -24 to 24
- gain_first: float32 [96], replicated, may hold values from 0.5 to 2
- gain_second: float32 [192], replicated, may hold values from 0.5 to 2
- conv_first: bfloat16 [3, 3, 3, 96, 192], replicated, may hold values from -0.125 to 0.125
- conv_second: bfloat16 [3, 3, 3, 192, 192], replicated, may hold values from -0.078125 to 0.078125
- shortcut: bfloat16 [96, 192], replicated, may hold values from -0.625 to 0.625
- downscale_weight: bfloat16 [3, 3, 192, 192], replicated, may hold values from -0.15625 to 0.15625
Outputs:
- encoded: bfloat16 [64, 32, 6144], P('tm', 'height', 'width')
The draws below stay inside these ranges and needn't reach their ends.
All inputs are finite; a program needn't handle non-finite values.
Results may differ from the reference program's by a relative error of at most 0.0054.
Values may be sent and summed in bfloat16 or wider, within the bound.
A program may use at most 64 MiB of HBM per device.

```python
import math
import jax
import jax.numpy as jnp
from jax import lax

C1 = 96
C2 = 192
FRAMES = 64
IMG_ROWS = 64
IMG_COLS = 64


def draw_video_in(key, part):
    key_base, key_chan, key_pos = jax.random.split(key, 3)
    chan_scale = jnp.exp(jax.random.uniform(key_chan, (C1,), jnp.float32, jnp.log(0.3), jnp.log(3.0)))
    pos_scale = jnp.exp(jax.random.uniform(key_pos, (FRAMES, IMG_ROWS, IMG_COLS, 1), jnp.float32, jnp.log(0.5), jnp.log(2.0)))
    base = jnp.clip(jax.random.normal(key_base, (FRAMES, IMG_ROWS, IMG_COLS, C1), jnp.float32), -4.0, 4.0)
    feature_values = base * chan_scale * pos_scale
    return feature_values.reshape(FRAMES, IMG_ROWS, IMG_COLS * C1).astype(jnp.bfloat16)


def scatter_about(own_key, shape, deviation, limit, kind=jnp.bfloat16):
    drawn = jax.random.normal(own_key, shape, jnp.float32) * deviation
    return jnp.minimum(jnp.maximum(drawn, -limit), limit).astype(kind)


def setup_inputs(seed: int = 0) -> dict:
    splits = jax.random.split(jax.random.key(seed), 8)
    video_in = draw_video_in(jax.random.fold_in(splits[7], 71), 0)
    gain_first = jnp.clip(jnp.exp(jax.random.uniform(splits[1], (C1,), jnp.float32, math.log(0.5), math.log(2.0))), 0.5, 2.0)
    gain_second = jnp.clip(jnp.exp(jax.random.uniform(splits[2], (C2,), jnp.float32, math.log(0.5), math.log(2.0))), 0.5, 2.0)
    conv_first = scatter_about(splits[3], (3, 3, 3, C1, C2), (27 * C1) ** -0.5, 0.125)
    conv_second = scatter_about(splits[4], (3, 3, 3, C2, C2), (27 * C2) ** -0.5, 0.078125)
    shortcut = scatter_about(splits[5], (C1, C2), C1 ** -0.5, 0.625)
    downscale_weight = scatter_about(splits[6], (3, 3, C2, C2), (9 * C2) ** -0.5, 0.15625)
    return dict(video_in=video_in, gain_first=gain_first, gain_second=gain_second, conv_first=conv_first, conv_second=conv_second, shortcut=shortcut, downscale_weight=downscale_weight)


epsilon = 1e-06

def activate(feature_values, gain):
    feature_values = feature_values.astype(jnp.float32)
    meansq = lax.optimization_barrier(jnp.mean(feature_values * feature_values, axis=-1, keepdims=True))
    normed = feature_values * lax.rsqrt(meansq + epsilon) * gain
    return jax.nn.silu(normed).astype(jnp.bfloat16)

def convolve(border_filled, filter_weight):
    frames = border_filled.shape[0] - 2
    rows = border_filled.shape[1] - 2
    cols = border_filled.shape[2] - 2
    c_in = border_filled.shape[3]
    c_out = filter_weight.shape[4]
    total = jnp.zeros((frames * rows * cols, c_out), jnp.float32)
    for depth_tap in range(3):
        for row_tap in range(3):
            window_slab = border_filled[depth_tap:depth_tap + frames, row_tap:row_tap + rows]
            stacked = jnp.concatenate([window_slab[:, :, col_tap:col_tap + cols] for col_tap in range(3)], axis=-1)
            total = total + jnp.dot(stacked.reshape(-1, 3 * c_in), filter_weight[depth_tap, row_tap].reshape(3 * c_in, c_out), preferred_element_type=jnp.float32)
    return total.reshape(frames, rows, cols, c_out)

def halve_spatial(border_filled, filter_weight):
    frames = border_filled.shape[0]
    out_rows = (border_filled.shape[1] - 1) // 2
    out_cols = (border_filled.shape[2] - 1) // 2
    chans = border_filled.shape[3]
    total = jnp.zeros((frames * out_rows * out_cols, filter_weight.shape[3]), jnp.float32)
    for row_tap in range(3):
        stacked = jnp.concatenate([border_filled[:, row_tap:row_tap + 2 * out_rows:2, col_tap:col_tap + 2 * out_cols:2] for col_tap in range(3)], axis=-1)
        total = total + jnp.dot(stacked.reshape(-1, 3 * chans), filter_weight[row_tap].reshape(3 * chans, filter_weight.shape[3]), preferred_element_type=jnp.float32)
    return total.reshape(frames, out_rows, out_cols, filter_weight.shape[3])

def reference(video_in, gain_first, gain_second, conv_first, conv_second, shortcut, downscale_weight):
    field = video_in.reshape(FRAMES, IMG_ROWS, IMG_COLS, C1)
    pads = ((2, 0), (1, 1), (1, 1), (0, 0))
    first = jnp.pad(activate(field, gain_first), pads)
    hidden = convolve(first, conv_first)
    second = jnp.pad(activate(hidden, gain_second), pads)
    branch = convolve(second, conv_second)
    skip_term = jnp.dot(field.reshape(-1, C1), shortcut, preferred_element_type=jnp.float32).reshape(FRAMES, IMG_ROWS, IMG_COLS, C2)
    merged = (branch + skip_term).astype(jnp.bfloat16)
    border_filled = jnp.pad(merged, ((0, 0), (0, 1), (0, 1), (0, 0)))
    block_output = halve_spatial(border_filled, downscale_weight)
    return block_output.astype(jnp.bfloat16).reshape(FRAMES, IMG_ROWS // 2, IMG_COLS // 2 * C2)
```

```python
import functools

import jax
import jax.numpy as jnp
from jax import lax
from jax.experimental import pallas as pl
from jax.experimental.pallas import tpu as pltpu
from jax.sharding import PartitionSpec as P

MESH = pl.DeviceIdType.MESH
epsilon = 1e-06
SIDES = [(-1, 0), (1, 0), (0, -1), (0, 1), (-1, -1), (-1, 1), (1, -1), (1, 1)]


def halo_kernel(x_ref, zb_ref, rb_ref, cl_ref, cr_ref, kl_ref, kr_ref, zs, zr, ss, sr):
    t, h, w = lax.axis_index("tm"), lax.axis_index("height"), lax.axis_index("width")
    nt, nh, nw = lax.axis_size("tm"), lax.axis_size("height"), lax.axis_size("width")

    def exists(dh, dw):
        ok = None
        for pos, by, n in ((h, dh, nh), (w, dw, nw)):
            if by:
                one = pos > 0 if by < 0 else pos < n - 1
                ok = one if ok is None else jnp.logical_and(ok, one)
        return ok

    def part(dh, dw):
        rows = {-1: pl.ds(0, 4), 0: pl.ds(0, 8), 1: pl.ds(6, 2)}[dh]
        lanes = {-1: pl.ds(0, 384), 0: pl.ds(0, 1536), 1: pl.ds(1152, 384)}[dw]
        return rows, lanes

    def landing(dh, dw):
        if dw == 0:
            return rb_ref, pl.ds(0, 1536)
        if dh == 0:
            return (cl_ref if dw == 1 else cr_ref), pl.ds(0, 384)
        return (kl_ref if dw == 1 else kr_ref), pl.ds(0, 384)

    bar = pltpu.get_barrier_semaphore()
    count = jnp.int32(0)
    for dh, dw in SIDES:
        ok = exists(dh, dw)
        count += ok.astype(jnp.int32)

        @pl.when(ok)
        def _():
            pl.semaphore_signal(bar, inc=1, device_id=(t, h + dh, w + dw), device_id_type=MESH)

    for dt in (-1, 1):
        ok = t > 0 if dt < 0 else t < nt - 1
        count += ok.astype(jnp.int32)

        @pl.when(ok)
        def _():
            pl.semaphore_signal(bar, inc=1, device_id=(t + dt, h, w), device_id_type=MESH)

    @pl.when(t == 0)
    def _():
        zb_ref[...] = jnp.zeros_like(zb_ref)
        for ref in (rb_ref, cl_ref, cr_ref, kl_ref, kr_ref):
            ref[pl.ds(0, 4)] = jnp.zeros((4,) + ref.shape[1:], ref.dtype)

    def clear(ref, rows, n):
        ref[:, pl.ds(rows, n), :] = jnp.zeros((8, n, ref.shape[2]), ref.dtype)

    @pl.when(h == 0)
    def _():
        for ref in (rb_ref, kl_ref, kr_ref):
            clear(ref, 6, 2)

    @pl.when(h == nh - 1)
    def _():
        for ref in (rb_ref, kl_ref, kr_ref):
            clear(ref, 0, 4)

    @pl.when(w == 0)
    def _():
        clear(cl_ref, 0, 8)
        clear(kl_ref, 0, 8)

    @pl.when(w == nw - 1)
    def _():
        clear(cr_ref, 0, 8)
        clear(kr_ref, 0, 8)

    pl.semaphore_wait(bar, count)

    def zcopy():
        return pltpu.make_async_remote_copy(
            src_ref=x_ref, dst_ref=zb_ref, send_sem=zs, recv_sem=zr,
            device_id=(t + 1, h, w), device_id_type=MESH)

    def scopy(i, half):
        dh, dw = SIDES[i]
        rows, lanes = part(dh, dw)
        dst, dlanes = landing(dh, dw)
        src = x_ref if half else zb_ref
        return pltpu.make_async_remote_copy(
            src_ref=src.at[:, rows, lanes], dst_ref=dst.at[pl.ds(4 * half, 4), rows, dlanes],
            send_sem=ss.at[half, i], recv_sem=sr.at[half, i],
            device_id=(t, h + dh, w + dw), device_id_type=MESH)

    @pl.when(t < nt - 1)
    def _():
        zcopy().start()

    for i, side in enumerate(SIDES):
        @pl.when(exists(*side))
        def _():
            scopy(i, 1).start()

    @pl.when(t > 0)
    def _():
        zcopy().wait_recv()
        for i, side in enumerate(SIDES):
            @pl.when(exists(*side))
            def _():
                scopy(i, 0).start()

    for half in (1, 0):
        for i, side in enumerate(SIDES):
            dh, dw = side
            here = exists(-dh, -dw)
            there = exists(dh, dw)
            if half == 0:
                here, there = jnp.logical_and(here, t > 0), jnp.logical_and(there, t > 0)

            @pl.when(here)
            def _():
                scopy(i, half).wait_recv()

            @pl.when(there)
            def _():
                scopy(i, half).wait_send()

    @pl.when(t < nt - 1)
    def _():
        zcopy().wait_send()


def gather_halo(x):
    shapes = [(4, 8, 1536), (8, 8, 1536)] + [(8, 8, 384)] * 4
    vm = pl.BlockSpec(memory_space=pltpu.VMEM)
    return pl.pallas_call(
        halo_kernel,
        out_shape=[jax.ShapeDtypeStruct(s, x.dtype) for s in shapes],
        in_specs=[pl.BlockSpec(memory_space=pl.ANY)],
        out_specs=[vm] * 6,
        scratch_shapes=[
            pltpu.SemaphoreType.DMA, pltpu.SemaphoreType.DMA,
            pltpu.SemaphoreType.DMA((2, 8)), pltpu.SemaphoreType.DMA((2, 8)),
        ],
        compiler_params=pltpu.CompilerParams(collective_id=0, has_side_effects=True),
    )(x)

def activate(v, gain, n):
    meansq = jnp.sum(v * v, axis=-1, keepdims=True) * (1.0 / n)
    half = v * lax.rsqrt(meansq + epsilon) * (0.5 * gain)
    return half + half * jnp.tanh(half)


def take_column(ref, first, col):
    tile, off = divmod(96 * col, 128)
    lane = lax.broadcasted_iota(jnp.int32, (32, 128), 1)

    def lanes(k):
        v = ref[pl.ds(first, 4), :, pl.ds(128 * k, 128)].astype(jnp.float32).reshape(32, 128)
        return pltpu.roll(v, 128 - off, 1) if off else v

    v = lanes(tile)
    if off + 96 > 128:
        v = jnp.where(lane < 128 - off, v, lanes(tile + 1))
    return jnp.where(lane < 96, v, 0.0)


def at(frame, row, col, rows):
    return (frame * rows + row) * 32 + 8 + col


def fill_first(group, blk, rb, cl, cr, kl, kr, gain, S, R):
    f0 = 4 * group

    def put(v, col, rim):
        a = activate(v, gain, 96)
        for k in range(4):
            e = f0 + k
            piece = a[8 * k : 8 * k + 8]
            raw = v[8 * k : 8 * k + 8]
            if rim:
                S[pl.ds(at(e, 10, col, 13), 3, stride=32), :] = piece[0:3]
                S[pl.ds(at(e, 0, col, 13), 2, stride=32), :] = piece[6:8]
            else:
                S[pl.ds(at(e, 2, col, 13), 8, stride=32), :] = piece
            if group == 1 and 0 <= col <= 16:
                if rim:
                    R[pl.ds(at(k, 8, col, 9), 1), :] = raw[0:1]
                else:
                    R[pl.ds(at(k, 0, col, 9), 8, stride=32), :] = raw

    for c in range(16):
        put(take_column(blk, 0, c), c, False)
        put(take_column(rb, f0, c), c, True)
    for c in (-2, -1):
        put(take_column(cl, f0, c + 4), c, False)
        put(take_column(kl, f0, c + 4), c, True)
    for c in (16, 17, 18):
        put(take_column(cr, f0, c - 16), c, False)
        put(take_column(kr, f0, c - 16), c, True)


def build_first(group, S, B1, E1):
    for e in range(4 * group, 4 * group + 4):
        for r in range(13):
            for dc in range(3):
                B1[dc, e, r] = S[pl.ds(at(e, r, dc - 1, 13), 16), :].astype(jnp.bfloat16)
        for dr in range(3):
            for k, c in enumerate((-2, -1, 0, 15, 16, 17, 18)):
                E1[dr, k, e] = S[pl.ds(at(e, dr, c, 13), 16, stride=32), :].astype(jnp.bfloat16)


def conv_first_frames(o, n, B1, E1, W1, gain, Ta, Tb):
    w = W1[...].reshape(27 * 128, 192)
    taps = [(dt, dr, dc) for dt in range(3) for dr in range(3) for dc in range(3)]
    for f in range(o, o + n):
        lhs = [B1[dc, f + dt, pl.ds(dr, 11)].reshape(176, 128) for dt, dr, dc in taps]
        for_ext = [
            jnp.concatenate([E1[dr, k + dc, f + dt] for k in (0, 3, 4)], axis=0) for dt, dr, dc in taps
        ]
        rows = [jnp.concatenate([m, x], axis=0) for m, x in zip(lhs, for_ext)]
        hidden = jnp.dot(jnp.concatenate(rows, axis=1), w, preferred_element_type=jnp.float32)
        second = activate(hidden, gain, 192)
        for r in range(11):
            Ta[pl.ds(at(f, r, 0, 11), 16), :] = second[16 * r : 16 * r + 16, 0:128]
            Tb[pl.ds(at(f, r, 0, 11), 16), 0:64] = second[16 * r : 16 * r + 16, 128:192]
        for k, c in enumerate((-1, 16, 17)):
            m = 176 + 16 * k
            Ta[pl.ds(at(f, 0, c, 11), 11, stride=32), :] = second[m : m + 11, 0:128]
            Tb[pl.ds(at(f, 0, c, 11), 11, stride=32), :] = jnp.concatenate(
                [second[m : m + 11, 128:192], jnp.zeros((11, 64), jnp.float32)], axis=1
            )


def mask_second(o, n, t, h, w, nh, nw, Ta, Tb):
    zero = jnp.zeros((32, 128), jnp.float32)

    def clear(f, r):
        for T in (Ta, Tb):
            T[pl.ds((f * 11 + r) * 32, 32), :] = zero

    @pl.when(h == 0)
    def _():
        for f in range(o, o + n):
            clear(f, 0)

    @pl.when(h == nh - 1)
    def _():
        for f in range(o, o + n):
            clear(f, 9)
            clear(f, 10)

    @pl.when(w == 0)
    def _():
        for f in range(o, o + n):
            for T in (Ta, Tb):
                T[pl.ds(at(f, 0, -1, 11), 11, stride=32), :] = zero[0:11]

    @pl.when(w == nw - 1)
    def _():
        for f in range(o, o + n):
            for T in (Ta, Tb):
                for c in (16, 17):
                    T[pl.ds(at(f, 0, c, 11), 11, stride=32), :] = zero[0:11]

    @pl.when(t == 0)
    def _():
        for f in range(o, min(o + n, 2)):
            for r in range(11):
                clear(f, r)


def build_second(o, n, Ta, Tb, B2, E2):
    for f in range(o, o + n):
        for r in range(11):
            for dc in range(3):
                s = pl.ds(at(f, r, dc - 1, 11), 16)
                B2[dc, f, r, :, 0:128] = Ta[s, :].astype(jnp.bfloat16)
                B2[dc, f, r, :, 128:256] = Tb[s, :].astype(jnp.bfloat16)
        for dr in range(3):
            for k, c in enumerate((15, 16, 17)):
                s = pl.ds(at(f, dr, c, 11), 16, stride=32)
                E2[dr, k, f, :, 0:128] = Ta[s, :].astype(jnp.bfloat16)
                E2[dr, k, f, :, 128:256] = Tb[s, :].astype(jnp.bfloat16)


def conv_second_frames(f, R, B2, E2, W2, WS, Mg):
    taps = [(dt, dr, dc) for dt in range(3) for dr in range(3) for dc in range(3)]
    rows = [
        jnp.concatenate([B2[dc, f + dt, pl.ds(dr, 9)].reshape(144, 256), E2[dr, dc, f + dt]], axis=0)
        for dt, dr, dc in taps
    ]
    raw = jnp.concatenate(
        [R[pl.ds(at(f, r, 0, 9), 16), :].astype(jnp.bfloat16) for r in range(9)]
        + [R[pl.ds(at(f, 0, 16, 9), 16, stride=32), :].astype(jnp.bfloat16)],
        axis=0,
    )
    merged = jnp.dot(
        jnp.concatenate(rows, axis=1), W2[...].reshape(27 * 256, 192), preferred_element_type=jnp.float32
    ) + jnp.dot(raw, WS[...], preferred_element_type=jnp.float32)
    merged = merged.astype(jnp.bfloat16).astype(jnp.float32)
    for r in range(9):
        Mg[0, pl.ds((f * 9 + r) * 32, 16), :] = merged[16 * r : 16 * r + 16, 0:128]
        Mg[1, pl.ds((f * 9 + r) * 32, 16), 0:64] = merged[16 * r : 16 * r + 16, 128:192]
    Mg[0, pl.ds(f * 288 + 16, 9, stride=32), :] = merged[144:153, 0:128]
    Mg[1, pl.ds(f * 288 + 16, 9, stride=32), :] = jnp.concatenate(
        [merged[144:153, 128:192], jnp.zeros((9, 64), jnp.float32)], axis=1
    )


def downscale(h, w, nh, nw, Mg, W3, Q, out_ref):
    zero = jnp.zeros((32, 128), jnp.float32)

    @pl.when(h == nh - 1)
    def _():
        for f in range(4):
            for p in range(2):
                Mg[p, pl.ds((f * 9 + 8) * 32, 32), :] = zero

    @pl.when(w == nw - 1)
    def _():
        for f in range(4):
            for p in range(2):
                Mg[p, pl.ds(f * 288 + 16, 9, stride=32), :] = zero[0:9]

    cols = []
    for dr in range(3):
        for dc in range(3):
            for p in range(2):
                cols.append(jnp.concatenate(
                    [Mg[p, pl.ds((f * 9 + 2 * i + dr) * 32 + dc, 8, stride=2), :]
                     for f in range(4) for i in range(4)], axis=0).astype(jnp.bfloat16))
    res = jnp.dot(
        jnp.concatenate(cols, axis=1), W3[...].reshape(9 * 256, 192), preferred_element_type=jnp.float32
    )
    Q[0] = res[:, 0:128]
    Q[1, :, 0:64] = res[:, 128:192]
    for f in range(4):
        for j in range(8):
            s = pl.ds(f * 32 + j, 4, stride=8)
            out_ref[f, :, 192 * j : 192 * j + 192] = jnp.concatenate(
                [Q[0, s, :], Q[1, s, :][:, 0:64]], axis=1
            ).astype(jnp.bfloat16)


def compute_kernel(x, zb, rb, cl, cr, kl, kr, g1, g2, k1, k2, sc, dw, out_ref,
                   S, R, B1, E1, Ta, Tb, B2, E2, Mg, Q, W1, W2, WS, W3, sem):
    t, h, w = lax.axis_index("tm"), lax.axis_index("height"), lax.axis_index("width")
    nh, nw = lax.axis_size("height"), lax.axis_size("width")
    loads = [
        pltpu.make_async_copy(k1, W1.at[:, pl.ds(0, 96), :], sem.at[0]),
        pltpu.make_async_copy(k2, W2.at[:, pl.ds(0, 192), :], sem.at[1]),
        pltpu.make_async_copy(sc, WS.at[pl.ds(0, 96), :], sem.at[2]),
        pltpu.make_async_copy(dw, W3.at[:, pl.ds(0, 192), :], sem.at[3]),
    ]
    for c in loads:
        c.start()
    W1[:, 96:128, :] = jnp.zeros((27, 32, 192), jnp.bfloat16)
    W2[:, 192:256, :] = jnp.zeros((27, 64, 192), jnp.bfloat16)
    WS[96:128, :] = jnp.zeros((32, 192), jnp.bfloat16)
    W3[:, 192:256, :] = jnp.zeros((9, 64, 192), jnp.bfloat16)
    Tb[...] = jnp.zeros_like(Tb)
    Mg[1] = jnp.zeros(Mg.shape[1:], jnp.float32)
    gain1 = jnp.concatenate([g1[...], jnp.zeros((1, 32), jnp.float32)], axis=1)
    gain2 = g2[...]

    fill_first(1, x, rb, cl, cr, kl, kr, gain1, S, R)
    build_first(1, S, B1, E1)
    loads[0].wait()
    conv_first_frames(4, 2, B1, E1, W1, gain2, Ta, Tb)
    mask_second(4, 2, t, h, w, nh, nw, Ta, Tb)
    build_second(4, 2, Ta, Tb, B2, E2)
    fill_first(0, zb, rb, cl, cr, kl, kr, gain1, S, R)
    build_first(0, S, B1, E1)
    conv_first_frames(0, 4, B1, E1, W1, gain2, Ta, Tb)
    mask_second(0, 4, t, h, w, nh, nw, Ta, Tb)
    build_second(0, 4, Ta, Tb, B2, E2)
    loads[1].wait()
    loads[2].wait()
    for f in range(4):
        conv_second_frames(f, R, B2, E2, W2, WS, Mg)
    loads[3].wait()
    downscale(h, w, nh, nw, Mg, W3, Q, out_ref)


COMPUTE_SCRATCH = [
    pltpu.VMEM(((8 * 13 + 8) * 32, 128), jnp.float32),
    pltpu.VMEM(((4 * 9 + 8) * 32, 128), jnp.float32),
    pltpu.VMEM((3, 8, 13, 16, 128), jnp.bfloat16),
    pltpu.VMEM((3, 7, 8, 16, 128), jnp.bfloat16),
    pltpu.VMEM(((6 * 11 + 8) * 32, 128), jnp.float32),
    pltpu.VMEM(((6 * 11 + 8) * 32, 128), jnp.float32),
    pltpu.VMEM((3, 6, 11, 16, 256), jnp.bfloat16),
    pltpu.VMEM((3, 3, 6, 16, 256), jnp.bfloat16),
    pltpu.VMEM((2, 4 * 9 * 32, 128), jnp.float32),
    pltpu.VMEM((2, 128, 128), jnp.float32),
    pltpu.VMEM((27, 128, 192), jnp.bfloat16),
    pltpu.VMEM((27, 256, 192), jnp.bfloat16),
    pltpu.VMEM((128, 192), jnp.bfloat16),
    pltpu.VMEM((9, 256, 192), jnp.bfloat16),
    pltpu.SemaphoreType.DMA((4,)),
]


def compute(x, halo, g1, g2, k1, k2, sc, dw):
    vm = pl.BlockSpec(memory_space=pltpu.VMEM)
    hbm = pl.BlockSpec(memory_space=pl.ANY)
    return pl.pallas_call(
        compute_kernel,
        out_shape=jax.ShapeDtypeStruct((4, 4, 1536), jnp.bfloat16),
        in_specs=[vm] * 9 + [hbm] * 4,
        out_specs=vm,
        scratch_shapes=COMPUTE_SCRATCH,
        compiler_params=pltpu.CompilerParams(vmem_limit_bytes=56 * 2**20),
    )(x, *halo, g1.reshape(1, 96), g2.reshape(1, 192), k1.reshape(27, 96, 192),
      k2.reshape(27, 192, 192), sc, dw.reshape(9, 192, 192))


def local(x, g1, g2, k1, k2, sc, dw):
    return compute(x, gather_halo(x), g1, g2, k1, k2, sc, dw)


def solution(mesh):
    placed = (P("tm", "height", "width"), P(), P(), P(), P(), P(), P())
    return jax.shard_map(
        local, mesh=mesh, in_specs=placed, out_specs=P("tm", "height", "width"), check_vma=False
    )
```

```python
import functools

import jax
import jax.numpy as jnp
from jax import lax
from jax.experimental import pallas as pl
from jax.experimental.pallas import tpu as pltpu
from jax.sharding import PartitionSpec as P

MESH = pl.DeviceIdType.MESH
epsilon = 1e-06
SIDES = [(-1, 0), (1, 0), (0, -1), (0, 1), (-1, -1), (-1, 1), (1, -1), (1, 1)]


class Halo:
    def __init__(self, x, zb, rb, cl, cr, kl, kr, zs, zr, ss, sr, credit):
        self.x, self.zb, self.rb, self.cl, self.cr, self.kl, self.kr = x, zb, rb, cl, cr, kl, kr
        self.zs, self.zr, self.ss, self.sr, self.credit = zs, zr, ss, sr, credit
        self.t, self.h, self.w = (lax.axis_index(a) for a in ("tm", "height", "width"))
        self.nt, self.nh, self.nw = (lax.axis_size(a) for a in ("tm", "height", "width"))

    def exists(self, dh, dw):
        ok = None
        for pos, by, n in ((self.h, dh, self.nh), (self.w, dw, self.nw)):
            if by:
                one = pos > 0 if by < 0 else pos < n - 1
                ok = one if ok is None else jnp.logical_and(ok, one)
        return ok

    def greet(self):
        t, h, w = self.t, self.h, self.w
        bar = pltpu.get_barrier_semaphore()
        for dh, dw in SIDES:
            @pl.when(self.exists(dh, dw))
            def _():
                pl.semaphore_signal(bar, inc=1, device_id=(t, h + dh, w + dw), device_id_type=MESH)

        @pl.when(t < self.nt - 1)
        def _():
            pl.semaphore_signal(bar, inc=1, device_id=(t + 1, h, w), device_id_type=MESH)

    def clear_outside(self):
        def clear(ref, rows, n):
            ref[:, pl.ds(rows, n), :] = jnp.zeros((8, n, ref.shape[2]), ref.dtype)

        @pl.when(self.t == 0)
        def _():
            self.zb[...] = jnp.zeros_like(self.zb)
            for ref in (self.rb, self.cl, self.cr, self.kl, self.kr):
                ref[pl.ds(0, 4)] = jnp.zeros((4,) + ref.shape[1:], ref.dtype)

        @pl.when(self.h == 0)
        def _():
            for ref in (self.rb, self.kl, self.kr):
                clear(ref, 6, 2)

        @pl.when(self.h == self.nh - 1)
        def _():
            for ref in (self.rb, self.kl, self.kr):
                clear(ref, 0, 4)

        @pl.when(self.w == 0)
        def _():
            clear(self.cl, 0, 8)
            clear(self.kl, 0, 8)

        @pl.when(self.w == self.nw - 1)
        def _():
            clear(self.cr, 0, 8)
            clear(self.kr, 0, 8)

    def meet(self):
        count = (self.t > 0).astype(jnp.int32)
        for side in SIDES:
            count += self.exists(*side).astype(jnp.int32)
        pl.semaphore_wait(pltpu.get_barrier_semaphore(), count)

        @pl.when(self.t > 0)
        def _():
            pl.semaphore_signal(
                self.credit, inc=1, device_id=(self.t - 1, self.h, self.w), device_id_type=MESH)

    def along(self):
        return pltpu.make_async_remote_copy(
            src_ref=self.x, dst_ref=self.zb, send_sem=self.zs, recv_sem=self.zr,
            device_id=(self.t + 1, self.h, self.w), device_id_type=MESH)

    def across(self, i, half):
        dh, dw = SIDES[i]
        rows = {-1: pl.ds(0, 4), 0: pl.ds(0, 8), 1: pl.ds(6, 2)}[dh]
        lanes = {-1: pl.ds(0, 384), 0: pl.ds(0, 1536), 1: pl.ds(1280, 256)}[dw]
        if dw == 0:
            dst = self.rb
        elif dh == 0:
            dst = self.cl if dw == 1 else self.cr
        else:
            dst = self.kl if dw == 1 else self.kr
        src = self.x if half else self.zb
        return pltpu.make_async_remote_copy(
            src_ref=src.at[:, rows, lanes], dst_ref=dst.at[pl.ds(4 * half, 4), rows],
            send_sem=self.ss.at[half, i], recv_sem=self.sr.at[half, i],
            device_id=(self.t, self.h + dh, self.w + dw), device_id_type=MESH)

    def send_across(self, half):
        for i, side in enumerate(SIDES):
            @pl.when(self.exists(*side))
            def _():
                self.across(i, half).start()

    def receive_across(self, half):
        for i, (dh, dw) in enumerate(SIDES):
            @pl.when(self.exists(-dh, -dw))
            def _():
                self.across(i, half).wait_recv()

    def sent_across(self, half):
        for i, side in enumerate(SIDES):
            @pl.when(self.exists(*side))
            def _():
                self.across(i, half).wait_send()

    def send_along(self):
        @pl.when(self.t < self.nt - 1)
        def _():
            pl.semaphore_wait(self.credit, 1)
            self.along().start()

    def relay(self):
        @pl.when(self.t > 0)
        def _():
            self.along().wait_recv()
            self.send_across(0)

    def receive_relayed(self):
        @pl.when(self.t > 0)
        def _():
            self.receive_across(0)

    def finish(self):
        self.sent_across(1)

        @pl.when(self.t > 0)
        def _():
            self.sent_across(0)

        @pl.when(self.t < self.nt - 1)
        def _():
            self.along().wait_send()


def activate(v, gain, n):
    meansq = jnp.sum(v * v, axis=-1, keepdims=True) * (1.0 / n)
    half = v * lax.rsqrt(meansq + epsilon) * (0.5 * gain)
    return half + half * jnp.tanh(half)


def take_column(ref, first, begin):
    tile, off = divmod(begin, 128)
    lane = lax.broadcasted_iota(jnp.int32, (32, 128), 1)

    def lanes(k):
        v = ref[pl.ds(first, 4), :, pl.ds(128 * k, 128)].astype(jnp.float32).reshape(32, 128)
        return pltpu.roll(v, 128 - off, 1) if off else v

    v = lanes(tile)
    if off + 96 > 128:
        v = jnp.where(lane < 128 - off, v, lanes(tile + 1))
    return jnp.where(lane < 96, v, 0.0)


def at(frame, row, col, rows):
    return (frame * rows + row) * 32 + 8 + col


def fill_first(group, part, blk, rb, cl, cr, kl, kr, gain, S, R):
    f0 = 4 * group

    def put(v, col, rim):
        a = activate(v, gain, 96)
        for k in range(4):
            e = f0 + k
            piece = a[8 * k : 8 * k + 8]
            raw = v[8 * k : 8 * k + 8]
            if rim:
                S[pl.ds(at(e, 10, col, 13), 3, stride=32), :] = piece[0:3]
                S[pl.ds(at(e, 0, col, 13), 2, stride=32), :] = piece[6:8]
            else:
                S[pl.ds(at(e, 2, col, 13), 8, stride=32), :] = piece
            if group == 1 and 0 <= col <= 16:
                if rim:
                    R[pl.ds(at(k, 8, col, 9), 1), :] = raw[0:1]
                else:
                    R[pl.ds(at(k, 0, col, 9), 8, stride=32), :] = raw

    if part == "block":
        for c in range(16):
            put(take_column(blk, 0, 96 * c), c, False)
        return
    for c in range(16):
        put(take_column(rb, f0, 96 * c), c, True)
    for c in (-2, -1):
        put(take_column(cl, f0, 64 + 96 * (c + 2)), c, False)
        put(take_column(kl, f0, 64 + 96 * (c + 2)), c, True)
    for c in (16, 17, 18):
        put(take_column(cr, f0, 96 * (c - 16)), c, False)
        put(take_column(kr, f0, 96 * (c - 16)), c, True)


def build_first(group, S, B1, E1):
    for e in range(4 * group, 4 * group + 4):
        for r in range(13):
            for dc in range(3):
                B1[dc, e, r] = S[pl.ds(at(e, r, dc - 1, 13), 16), :].astype(jnp.bfloat16)
        for dr in range(3):
            for k, c in enumerate((-2, -1, 0, 15, 16, 17, 18)):
                E1[dr, k, e] = S[pl.ds(at(e, dr, c, 13), 16, stride=32), :].astype(jnp.bfloat16)


def conv_first_frames(o, n, B1, E1, W1, gain, Ta, Tb):
    w = W1[...].reshape(27 * 128, 192)
    taps = [(dt, dr, dc) for dt in range(3) for dr in range(3) for dc in range(3)]
    for f in range(o, o + n):
        lhs = [B1[dc, f + dt, pl.ds(dr, 11)].reshape(176, 128) for dt, dr, dc in taps]
        for_ext = [
            jnp.concatenate([E1[dr, k + dc, f + dt] for k in (0, 3, 4)], axis=0) for dt, dr, dc in taps
        ]
        rows = [jnp.concatenate([m, x], axis=0) for m, x in zip(lhs, for_ext)]
        hidden = jnp.dot(jnp.concatenate(rows, axis=1), w, preferred_element_type=jnp.float32)
        second = activate(hidden, gain, 192)
        for r in range(11):
            Ta[pl.ds(at(f, r, 0, 11), 16), :] = second[16 * r : 16 * r + 16, 0:128]
            Tb[pl.ds(at(f, r, 0, 11), 16), 0:64] = second[16 * r : 16 * r + 16, 128:192]
        for k, c in enumerate((-1, 16, 17)):
            m = 176 + 16 * k
            Ta[pl.ds(at(f, 0, c, 11), 11, stride=32), :] = second[m : m + 11, 0:128]
            Tb[pl.ds(at(f, 0, c, 11), 11, stride=32), :] = jnp.concatenate(
                [second[m : m + 11, 128:192], jnp.zeros((11, 64), jnp.float32)], axis=1
            )


def mask_second(o, n, t, h, w, nh, nw, Ta, Tb):
    zero = jnp.zeros((32, 128), jnp.float32)

    def clear(f, r):
        for T in (Ta, Tb):
            T[pl.ds((f * 11 + r) * 32, 32), :] = zero

    @pl.when(h == 0)
    def _():
        for f in range(o, o + n):
            clear(f, 0)

    @pl.when(h == nh - 1)
    def _():
        for f in range(o, o + n):
            clear(f, 9)
            clear(f, 10)

    @pl.when(w == 0)
    def _():
        for f in range(o, o + n):
            for T in (Ta, Tb):
                T[pl.ds(at(f, 0, -1, 11), 11, stride=32), :] = zero[0:11]

    @pl.when(w == nw - 1)
    def _():
        for f in range(o, o + n):
            for T in (Ta, Tb):
                for c in (16, 17):
                    T[pl.ds(at(f, 0, c, 11), 11, stride=32), :] = zero[0:11]

    @pl.when(t == 0)
    def _():
        for f in range(o, min(o + n, 2)):
            for r in range(11):
                clear(f, r)


def build_second(o, n, Ta, Tb, B2, E2):
    for f in range(o, o + n):
        for r in range(11):
            for dc in range(3):
                s = pl.ds(at(f, r, dc - 1, 11), 16)
                B2[dc, f, r, :, 0:128] = Ta[s, :].astype(jnp.bfloat16)
                B2[dc, f, r, :, 128:256] = Tb[s, :].astype(jnp.bfloat16)
        for dr in range(3):
            for k, c in enumerate((15, 16, 17)):
                s = pl.ds(at(f, dr, c, 11), 16, stride=32)
                E2[dr, k, f, :, 0:128] = Ta[s, :].astype(jnp.bfloat16)
                E2[dr, k, f, :, 128:256] = Tb[s, :].astype(jnp.bfloat16)


def conv_second_frames(f, R, B2, E2, W2, WS, Mg):
    taps = [(dt, dr, dc) for dt in range(3) for dr in range(3) for dc in range(3)]
    rows = [
        jnp.concatenate([B2[dc, f + dt, pl.ds(dr, 9)].reshape(144, 256), E2[dr, dc, f + dt]], axis=0)
        for dt, dr, dc in taps
    ]
    raw = jnp.concatenate(
        [R[pl.ds(at(f, r, 0, 9), 16), :].astype(jnp.bfloat16) for r in range(9)]
        + [R[pl.ds(at(f, 0, 16, 9), 16, stride=32), :].astype(jnp.bfloat16)],
        axis=0,
    )
    merged = jnp.dot(
        jnp.concatenate(rows, axis=1), W2[...].reshape(27 * 256, 192), preferred_element_type=jnp.float32
    ) + jnp.dot(raw, WS[...], preferred_element_type=jnp.float32)
    merged = merged.astype(jnp.bfloat16).astype(jnp.float32)
    for r in range(9):
        Mg[0, pl.ds((f * 9 + r) * 32, 16), :] = merged[16 * r : 16 * r + 16, 0:128]
        Mg[1, pl.ds((f * 9 + r) * 32, 16), 0:64] = merged[16 * r : 16 * r + 16, 128:192]
    Mg[0, pl.ds(f * 288 + 16, 9, stride=32), :] = merged[144:153, 0:128]
    Mg[1, pl.ds(f * 288 + 16, 9, stride=32), :] = jnp.concatenate(
        [merged[144:153, 128:192], jnp.zeros((9, 64), jnp.float32)], axis=1
    )


def clear_merged(h, w, nh, nw, Mg):
    zero = jnp.zeros((32, 128), jnp.float32)

    @pl.when(h == nh - 1)
    def _():
        for f in range(4):
            for p in range(2):
                Mg[p, pl.ds((f * 9 + 8) * 32, 32), :] = zero

    @pl.when(w == nw - 1)
    def _():
        for f in range(4):
            for p in range(2):
                Mg[p, pl.ds(f * 288 + 16, 9, stride=32), :] = zero[0:9]


def downscale(Mg, W3, Q, out_ref):
    cols = []
    for dr in range(3):
        for dc in range(3):
            for p in range(2):
                cols.append(jnp.concatenate(
                    [Mg[p, pl.ds((f * 9 + 2 * i + dr) * 32 + dc, 8, stride=2), :]
                     for f in range(4) for i in range(4)], axis=0).astype(jnp.bfloat16))
    res = jnp.dot(
        jnp.concatenate(cols, axis=1), W3[...].reshape(9 * 256, 192), preferred_element_type=jnp.float32
    )
    Q[0] = res[:, 0:128]
    Q[1, :, 0:64] = res[:, 128:192]
    for f in range(4):
        for j in range(8):
            s = pl.ds(f * 32 + j, 4, stride=8)
            out_ref[f, :, 192 * j : 192 * j + 192] = jnp.concatenate(
                [Q[0, s, :], Q[1, s, :][:, 0:64]], axis=1
            ).astype(jnp.bfloat16)


def field_kernel(x, g1, g2, k1, k2, sc, k3, out, zb, rb, cl, cr, kl, kr,
                 xs, ga, gb, S, R, B1, E1, Ta, Tb, B2, E2, W1, W2, WS, W3, Mg, Q,
                 sem, zs, zr, ss, sr, credit):
    halo = Halo(x, zb, rb, cl, cr, kl, kr, zs, zr, ss, sr, credit)
    t, h, w, nh, nw = halo.t, halo.h, halo.w, halo.nh, halo.nw
    rims = (rb, cl, cr, kl, kr)
    halo.greet()
    loads = [
        pltpu.make_async_copy(x, xs, sem.at[0]),
        pltpu.make_async_copy(k1, W1.at[:, pl.ds(0, 96), :], sem.at[1]),
        pltpu.make_async_copy(k2, W2.at[:, pl.ds(0, 192), :], sem.at[2]),
        pltpu.make_async_copy(sc, WS.at[pl.ds(0, 96), :], sem.at[3]),
        pltpu.make_async_copy(g1, ga, sem.at[4]),
        pltpu.make_async_copy(g2, gb, sem.at[5]),
        pltpu.make_async_copy(k3, W3.at[:, pl.ds(0, 192), :], sem.at[6]),
    ]
    for c in loads:
        c.start()
    halo.clear_outside()
    halo.meet()
    halo.send_across(1)
    W1[:, 96:128, :] = jnp.zeros((27, 32, 192), jnp.bfloat16)
    W2[:, 192:256, :] = jnp.zeros((27, 64, 192), jnp.bfloat16)
    W3[:, 192:256, :] = jnp.zeros((9, 64, 192), jnp.bfloat16)
    WS[96:128, :] = jnp.zeros((32, 192), jnp.bfloat16)
    Tb[...] = jnp.zeros_like(Tb)
    Mg[1] = jnp.zeros(Mg.shape[1:], jnp.float32)
    loads[0].wait()
    loads[4].wait()
    loads[5].wait()
    gain1 = jnp.concatenate([ga[...], jnp.zeros((1, 32), jnp.float32)], axis=1)
    gain2 = gb[...]
    fill_first(1, "block", xs, *rims, gain1, S, R)
    halo.send_along()
    halo.relay()
    halo.receive_across(1)
    fill_first(1, "rims", xs, *rims, gain1, S, R)
    build_first(1, S, B1, E1)
    loads[1].wait()
    conv_first_frames(4, 2, B1, E1, W1, gain2, Ta, Tb)
    mask_second(4, 2, t, h, w, nh, nw, Ta, Tb)
    build_second(4, 2, Ta, Tb, B2, E2)
    fill_first(0, "block", zb, *rims, gain1, S, R)
    halo.receive_relayed()
    fill_first(0, "rims", zb, *rims, gain1, S, R)
    build_first(0, S, B1, E1)
    conv_first_frames(0, 4, B1, E1, W1, gain2, Ta, Tb)
    mask_second(0, 4, t, h, w, nh, nw, Ta, Tb)
    build_second(0, 4, Ta, Tb, B2, E2)
    loads[2].wait()
    loads[3].wait()
    for f in range(4):
        conv_second_frames(f, R, B2, E2, W2, WS, Mg)
    clear_merged(h, w, nh, nw, Mg)
    loads[6].wait()
    downscale(Mg, W3, Q, out)
    halo.finish()


VM = pl.BlockSpec(memory_space=pltpu.VMEM)
HBM = pl.BlockSpec(memory_space=pltpu.HBM)
LANDING = [(4, 8, 1536), (8, 8, 1536), (8, 8, 256), (8, 8, 384), (8, 8, 256), (8, 8, 384)]


def field(x, g1, g2, k1, k2, sc, k3):
    bf, f32, dma = jnp.bfloat16, jnp.float32, pltpu.SemaphoreType.DMA
    shapes = [
        ((4, 8, 1536), bf), ((1, 96), f32), ((1, 192), f32),
        (((8 * 13 + 8) * 32, 128), f32), (((4 * 9 + 8) * 32, 128), f32),
        ((3, 8, 13, 16, 128), bf), ((3, 7, 8, 16, 128), bf),
        (((6 * 11 + 8) * 32, 128), f32), (((6 * 11 + 8) * 32, 128), f32),
        ((3, 6, 11, 16, 256), bf), ((3, 3, 6, 16, 256), bf),
        ((27, 128, 192), bf), ((27, 256, 192), bf), ((128, 192), bf), ((9, 256, 192), bf),
        ((2, 4 * 9 * 32, 128), f32), ((2, 128, 128), f32),
    ]
    return pl.pallas_call(
        field_kernel,
        out_shape=[jax.ShapeDtypeStruct((4, 4, 1536), bf)] + [jax.ShapeDtypeStruct(s, bf) for s in LANDING],
        in_specs=[HBM] * 7,
        out_specs=[VM] * 7,
        scratch_shapes=[pltpu.VMEM(*s) for s in shapes]
        + [dma((7,)), dma, dma, dma((2, 8)), dma((2, 8)), pltpu.SemaphoreType.REGULAR],
        compiler_params=pltpu.CompilerParams(
            collective_id=0, has_side_effects=True, vmem_limit_bytes=60 * 2**20),
    )(x, g1.reshape(1, 96), g2.reshape(1, 192), k1.reshape(27, 96, 192), k2.reshape(27, 192, 192), sc,
      k3.reshape(9, 192, 192))[0]


def local(x, g1, g2, k1, k2, sc, dw):
    return field(x, g1, g2, k1, k2, sc, dw)


def solution(mesh):
    placed = (P("tm", "height", "width"), P(), P(), P(), P(), P(), P())
    return jax.shard_map(
        local, mesh=mesh, in_specs=placed, out_specs=P("tm", "height", "width"), check_vma=False
    )
```

```python
import functools

import jax
import jax.numpy as jnp
from jax import lax
from jax.experimental import pallas as pl
from jax.experimental.pallas import tpu as pltpu
from jax.sharding import PartitionSpec as P

MESH = pl.DeviceIdType.MESH
epsilon = 1e-06
SIDES = [(-1, 0), (1, 0), (0, -1), (0, 1), (-1, -1), (-1, 1), (1, -1), (1, 1)]


class Halo:
    def __init__(self, x, zb, rb, cl, cr, kl, kr, zs, zr, ss, sr, credit):
        self.x, self.zb, self.rb, self.cl, self.cr, self.kl, self.kr = x, zb, rb, cl, cr, kl, kr
        self.zs, self.zr, self.ss, self.sr, self.credit = zs, zr, ss, sr, credit
        self.t, self.h, self.w = (lax.axis_index(a) for a in ("tm", "height", "width"))
        self.nt, self.nh, self.nw = (lax.axis_size(a) for a in ("tm", "height", "width"))

    def exists(self, dh, dw):
        ok = None
        for pos, by, n in ((self.h, dh, self.nh), (self.w, dw, self.nw)):
            if by:
                one = pos > 0 if by < 0 else pos < n - 1
                ok = one if ok is None else jnp.logical_and(ok, one)
        return ok

    def greet(self):
        t, h, w = self.t, self.h, self.w
        bar = pltpu.get_barrier_semaphore()
        for dh, dw in SIDES:
            @pl.when(self.exists(dh, dw))
            def _():
                pl.semaphore_signal(bar, inc=1, device_id=(t, h + dh, w + dw), device_id_type=MESH)

        @pl.when(t < self.nt - 1)
        def _():
            pl.semaphore_signal(bar, inc=1, device_id=(t + 1, h, w), device_id_type=MESH)

    def clear_outside(self):
        def clear(ref, rows, n):
            ref[:, pl.ds(rows, n), :] = jnp.zeros((8, n, ref.shape[2]), ref.dtype)

        @pl.when(self.t == 0)
        def _():
            self.zb[...] = jnp.zeros_like(self.zb)
            for ref in (self.rb, self.cl, self.cr, self.kl, self.kr):
                ref[pl.ds(0, 4)] = jnp.zeros((4,) + ref.shape[1:], ref.dtype)

        @pl.when(self.h == 0)
        def _():
            for ref in (self.rb, self.kl, self.kr):
                clear(ref, 6, 2)

        @pl.when(self.h == self.nh - 1)
        def _():
            for ref in (self.rb, self.kl, self.kr):
                clear(ref, 0, 4)

        @pl.when(self.w == 0)
        def _():
            clear(self.cl, 0, 8)
            clear(self.kl, 0, 8)

        @pl.when(self.w == self.nw - 1)
        def _():
            clear(self.cr, 0, 8)
            clear(self.kr, 0, 8)

    def meet(self):
        count = (self.t > 0).astype(jnp.int32)
        for side in SIDES:
            count += self.exists(*side).astype(jnp.int32)
        pl.semaphore_wait(pltpu.get_barrier_semaphore(), count)

        @pl.when(self.t > 0)
        def _():
            pl.semaphore_signal(
                self.credit, inc=1, device_id=(self.t - 1, self.h, self.w), device_id_type=MESH)

    def along(self):
        return pltpu.make_async_remote_copy(
            src_ref=self.x, dst_ref=self.zb, send_sem=self.zs, recv_sem=self.zr,
            device_id=(self.t + 1, self.h, self.w), device_id_type=MESH)

    def across(self, i, half):
        dh, dw = SIDES[i]
        rows = {-1: pl.ds(0, 4), 0: pl.ds(0, 8), 1: pl.ds(6, 2)}[dh]
        lanes = {-1: pl.ds(0, 384), 0: pl.ds(0, 1536), 1: pl.ds(1280, 256)}[dw]
        if dw == 0:
            dst = self.rb
        elif dh == 0:
            dst = self.cl if dw == 1 else self.cr
        else:
            dst = self.kl if dw == 1 else self.kr
        src = self.x if half else self.zb
        return pltpu.make_async_remote_copy(
            src_ref=src.at[:, rows, lanes], dst_ref=dst.at[pl.ds(4 * half, 4), rows],
            send_sem=self.ss.at[half, i], recv_sem=self.sr.at[half, i],
            device_id=(self.t, self.h + dh, self.w + dw), device_id_type=MESH)

    def send_across(self, half):
        for i, side in enumerate(SIDES):
            @pl.when(self.exists(*side))
            def _():
                self.across(i, half).start()

    def receive_across(self, half):
        for i, (dh, dw) in enumerate(SIDES):
            @pl.when(self.exists(-dh, -dw))
            def _():
                self.across(i, half).wait_recv()

    def sent_across(self, half):
        for i, side in enumerate(SIDES):
            @pl.when(self.exists(*side))
            def _():
                self.across(i, half).wait_send()

    def send_along(self):
        @pl.when(self.t < self.nt - 1)
        def _():
            pl.semaphore_wait(self.credit, 1)
            self.along().start()

    def relay(self):
        @pl.when(self.t > 0)
        def _():
            self.along().wait_recv()
            self.send_across(0)

    def receive_relayed(self):
        @pl.when(self.t > 0)
        def _():
            self.receive_across(0)

    def finish(self):
        self.sent_across(1)

        @pl.when(self.t > 0)
        def _():
            self.sent_across(0)

        @pl.when(self.t < self.nt - 1)
        def _():
            self.along().wait_send()


def activate(v, gain, n):
    meansq = jnp.sum(v * v, axis=-1, keepdims=True) * (1.0 / n)
    half = v * lax.rsqrt(meansq + epsilon) * (0.5 * gain)
    return half + half * jnp.tanh(half)


def take_column(ref, first, begin):
    tile, off = divmod(begin, 128)
    lane = lax.broadcasted_iota(jnp.int32, (32, 128), 1)

    def lanes(k):
        v = ref[pl.ds(first, 4), :, pl.ds(128 * k, 128)].astype(jnp.float32).reshape(32, 128)
        return pltpu.roll(v, 128 - off, 1) if off else v

    v = lanes(tile)
    if off + 96 > 128:
        v = jnp.where(lane < 128 - off, v, lanes(tile + 1))
    return jnp.where(lane < 96, v, 0.0)


def at(frame, row, col, rows):
    return (frame * rows + row) * 32 + 8 + col


def fill_first(group, part, blk, rb, cl, cr, kl, kr, gain, S, R):
    f0 = 4 * group

    def put(v, col, rim):
        a = activate(v, gain, 96)
        for k in range(4):
            e = f0 + k
            piece = a[8 * k : 8 * k + 8]
            raw = v[8 * k : 8 * k + 8]
            if rim:
                S[pl.ds(at(e, 10, col, 13), 3, stride=32), :] = piece[0:3]
                S[pl.ds(at(e, 0, col, 13), 2, stride=32), :] = piece[6:8]
            else:
                S[pl.ds(at(e, 2, col, 13), 8, stride=32), :] = piece
            if group == 1 and 0 <= col <= 16:
                if rim:
                    R[pl.ds(at(k, 8, col, 9), 1), :] = raw[0:1]
                else:
                    R[pl.ds(at(k, 0, col, 9), 8, stride=32), :] = raw

    if part == "block":
        for c in range(16):
            put(take_column(blk, 0, 96 * c), c, False)
        return
    for c in range(16):
        put(take_column(rb, f0, 96 * c), c, True)
    for c in (-2, -1):
        put(take_column(cl, f0, 64 + 96 * (c + 2)), c, False)
        put(take_column(kl, f0, 64 + 96 * (c + 2)), c, True)
    for c in (16, 17, 18):
        put(take_column(cr, f0, 96 * (c - 16)), c, False)
        put(take_column(kr, f0, 96 * (c - 16)), c, True)


def build_first(group, S, B1, E1):
    for e in range(4 * group, 4 * group + 4):
        for r in range(13):
            for dc in range(3):
                B1[dc, e, r] = S[pl.ds(at(e, r, dc - 1, 13), 16), :].astype(jnp.bfloat16)
        for dr in range(3):
            for k, c in enumerate((-2, -1, 0, 15, 16, 17, 18)):
                E1[dr, k, e] = S[pl.ds(at(e, dr, c, 13), 16, stride=32), :].astype(jnp.bfloat16)


TAPS = [(dr, dc) for dr in range(3) for dc in range(3)]


class Keep:
    def __init__(self, h, w, nh, nw):
        f32 = jnp.float32
        self.top, self.bottom = (h > 0).astype(f32), (h < nh - 1).astype(f32)
        self.left, self.right = (w > 0).astype(f32), (w < nw - 1).astype(f32)

    def rows(self, first_below, top):
        row = lax.broadcasted_iota(jnp.int32, (16, 128), 0)
        m = jnp.where(row >= first_below, self.bottom, 1.0)
        return jnp.where(row == 0, self.top, m) if top else m


def conv_first(o, lo, hi, B1, E1, W1):
    rows = [
        jnp.concatenate(
            [B1[dc, o + dt, pl.ds(dr, 11)].reshape(176, 128)] + [E1[dr, k + dc, o + dt] for k in (0, 3, 4)], axis=0)
        for dt in range(lo, hi) for dr, dc in TAPS
    ]
    w = W1[pl.ds(9 * lo, 9 * (hi - lo))].reshape((hi - lo) * 9 * 128, 192)
    return jnp.dot(jnp.concatenate(rows, axis=1), w, preferred_element_type=jnp.float32)


def put_second(f, hidden, gain, keep, Ta, Tb):
    second = activate(hidden, gain, 192)
    pa = second[:, 0:128]
    pb = jnp.concatenate([second[:, 128:192], second[:, 128:192]], axis=1)
    for r in range(11):
        for T, p in ((Ta, pa), (Tb, pb)):
            v = p[16 * r : 16 * r + 16]
            if r == 0:
                v = v * keep.top
            if r >= 9:
                v = v * keep.bottom
            T[pl.ds(at(f, r, 0, 11), 16), :] = v
    inside = keep.rows(9, True)
    for k, c in enumerate((-1, 16, 17)):
        m = 176 + 16 * k
        side = inside * (keep.left if k == 0 else keep.right)
        for T, p in ((Ta, pa), (Tb, pb)):
            T[pl.ds(at(f, 0, c, 11), 11, stride=32), :] = (p[m : m + 16] * side)[0:11]


def halves(a, b):
    lane = lax.broadcasted_iota(jnp.int32, a.shape, 1)
    return jnp.where(lane < 64, a, b).astype(jnp.bfloat16)


def build_second(f, Ta, Tb, A2, P01, P2r, D2, A2e, P01e, P2re, D2e):
    for r in range(11):
        spans = [pl.ds(at(f, r, dc - 1, 11), 16) for dc in range(3)]
        for dc in range(3):
            A2[dc, f, r] = Ta[spans[dc], :].astype(jnp.bfloat16)
        P01[f, r] = halves(Tb[spans[0], :], Tb[spans[1], :])
        if r < 9:
            P2r[f, r] = halves(Tb[spans[2], :], Tb[pl.ds(at(f, r + 1, 1, 11), 16), :])
        if r >= 2:
            D2[f, r - 2] = Tb[spans[2], :].astype(jnp.bfloat16)
    for dr in range(3):
        spans = [pl.ds(at(f, dr, c, 11), 16, stride=32) for c in (15, 16, 17)]
        for k in range(3):
            A2e[dr, k, f] = Ta[spans[k], :].astype(jnp.bfloat16)
        P01e[dr, f] = halves(Tb[spans[0], :], Tb[spans[1], :])
    rows = [Tb[pl.ds(at(f, dr, 17, 11), 16, stride=32), :] for dr in range(3)]
    P2re[f] = halves(rows[0], rows[1])
    D2e[f] = rows[2].astype(jnp.bfloat16)


def build_pair(f, Tb, P2f, P2fe):
    for r in range(2, 11):
        P2f[f, r - 2] = halves(Tb[pl.ds(at(f, r, 1, 11), 16), :], Tb[pl.ds(at(f + 1, r, 1, 11), 16), :])
    P2fe[f] = halves(*(Tb[pl.ds(at(g, 2, 17, 11), 16, stride=32), :] for g in (f, f + 1)))


BASE = (0, 14, 27)


def tile_of(dt, dr, dc):
    if dc < 2:
        return BASE[dt] + 9 + dr, dc
    if dr < 2:
        return BASE[dt] + 12, dr
    return (13, dt) if dt < 2 else (40, 0)


def conv_second(f, first, last, ops, W2):
    A2, P01, P2r, D2, A2e, P01e, P2re, D2e, P2f, P2fe, R = ops

    def tile(i):
        if i == 41:
            return [R[pl.ds(at(f, r, 0, 9), 16), :].astype(jnp.bfloat16) for r in range(9)] + [
                R[pl.ds(at(f, 0, 16, 9), 16, stride=32), :].astype(jnp.bfloat16)]
        if i == 13:
            return [P2f[f].reshape(144, 128), P2fe[f]]
        if i == 40:
            return [D2[f + 2].reshape(144, 128), D2e[f + 2]]
        dt = 2 if i >= BASE[2] else 1 if i >= BASE[1] else 0
        k, g = i - BASE[dt], f + dt
        if k < 9:
            dr, dc = TAPS[k]
            return [A2[dc, g, pl.ds(dr, 9)].reshape(144, 128), A2e[dr, dc, g]]
        if k < 12:
            return [P01[g, pl.ds(k - 9, 9)].reshape(144, 128), P01e[k - 9, g]]
        return [P2r[g].reshape(144, 128), P2re[g]]

    lhs = jnp.concatenate([jnp.concatenate(tile(i), axis=0) for i in range(first, last)], axis=1)
    w = W2[pl.ds(first, last - first)].reshape((last - first) * 128, 192)
    return jnp.dot(lhs, w, preferred_element_type=jnp.float32)


def put_merged(f, merged, keep, Mg):
    merged = merged.astype(jnp.bfloat16).astype(jnp.float32)
    pb = jnp.concatenate([merged[:, 128:192], jnp.zeros((160, 64), jnp.float32)], axis=1)
    side = keep.rows(8, False) * keep.right
    for p, v in enumerate((merged[:, 0:128], pb)):
        for r in range(9):
            part = v[16 * r : 16 * r + 16]
            Mg[p, pl.ds((f * 9 + r) * 32, 16), :] = part * keep.bottom if r == 8 else part
        Mg[p, pl.ds(f * 288 + 16, 9, stride=32), :] = (v[144:160] * side)[0:9]


def downscale(Mg, W3, Q, out_ref):
    cols = []
    for dr in range(3):
        for dc in range(3):
            for p in range(2):
                cols.append(jnp.concatenate(
                    [Mg[p, pl.ds((f * 9 + 2 * i + dr) * 32 + dc, 8, stride=2), :]
                     for f in range(4) for i in range(4)], axis=0).astype(jnp.bfloat16))
    res = jnp.dot(
        jnp.concatenate(cols, axis=1), W3[...].reshape(9 * 256, 192), preferred_element_type=jnp.float32
    )
    Q[0] = res[:, 0:128]
    Q[1, :, 0:64] = res[:, 128:192]
    for f in range(4):
        for j in range(8):
            s = pl.ds(f * 32 + j, 4, stride=8)
            out_ref[f, :, 192 * j : 192 * j + 192] = jnp.concatenate(
                [Q[0, s, :], Q[1, s, :][:, 0:64]], axis=1
            ).astype(jnp.bfloat16)


def field_kernel(x, g1, g2, k1, k2, sc, k3, out, zb, rb, cl, cr, kl, kr,
                 xs, ga, gb, S, R, B1, E1, Ta, Tb, A2, P01, P2r, D2, A2e, P01e, P2re, D2e, P2f, P2fe,
                 W1, W2, W3, Mg, Q, acc1, acc2, sem, wsem, zs, zr, ss, sr, credit):
    halo = Halo(x, zb, rb, cl, cr, kl, kr, zs, zr, ss, sr, credit)
    rims = (rb, cl, cr, kl, kr)
    halo.greet()
    loads = [
        pltpu.make_async_copy(x, xs, sem.at[0]),
        pltpu.make_async_copy(g1, ga, sem.at[1]),
        pltpu.make_async_copy(g2, gb, sem.at[2]),
        pltpu.make_async_copy(k1, W1.at[:, pl.ds(0, 96), :], sem.at[3]),
        pltpu.make_async_copy(k3, W3.at[:, pl.ds(0, 192), :], sem.at[4]),
    ]
    loads2 = [pltpu.make_async_copy(sc, W2.at[41, pl.ds(0, 96), :], wsem.at[30])]
    for dt in range(3):
        loads2.append(pltpu.make_async_copy(
            k2.at[pl.ds(9 * dt, 9), pl.ds(0, 128), :], W2.at[pl.ds(BASE[dt], 9)], wsem.at[27 + dt]))
        for n, (dr, dc) in enumerate(TAPS):
            i, half = tile_of(dt, dr, dc)
            loads2.append(pltpu.make_async_copy(
                k2.at[9 * dt + n, pl.ds(128, 64), :], W2.at[i, pl.ds(64 * half, 64), :], wsem.at[9 * dt + n]))
    for c in loads:
        c.start()
    halo.clear_outside()
    halo.meet()
    halo.send_across(1)
    for c in loads2:
        c.start()
    W1[:, 96:128, :] = jnp.zeros((27, 32, 192), jnp.bfloat16)
    W2[40, 64:128, :] = jnp.zeros((64, 192), jnp.bfloat16)
    W2[41, 96:128, :] = jnp.zeros((32, 192), jnp.bfloat16)
    W3[:, 192:256, :] = jnp.zeros((9, 64, 192), jnp.bfloat16)
    Mg[1] = jnp.zeros(Mg.shape[1:], jnp.float32)
    for c in loads[:3]:
        c.wait()
    gain1 = jnp.concatenate([ga[...], jnp.zeros((1, 32), jnp.float32)], axis=1)
    gain2 = gb[...]
    keep = Keep(halo.h, halo.w, halo.nh, halo.nw)
    ops = (A2, P01, P2r, D2, A2e, P01e, P2re, D2e)
    all_ops = ops + (P2f, P2fe, R)

    fill_first(1, "block", xs, *rims, gain1, S, R)
    halo.send_along()
    halo.relay()
    halo.receive_across(1)
    loads[3].wait()
    fill_first(1, "rims", xs, *rims, gain1, S, R)
    build_first(1, S, B1, E1)
    for o in (4, 5):
        put_second(o, conv_first(o, 0, 3, B1, E1, W1), gain2, keep, Ta, Tb)
    fill_first(0, "block", zb, *rims, gain1, S, R)
    acc1[0] = conv_first(2, 2, 3, B1, E1, W1)
    acc1[1] = conv_first(3, 1, 3, B1, E1, W1)
    for o in (4, 5):
        build_second(o, Ta, Tb, *ops)
    for c in loads2:
        c.wait()
    acc2[0] = conv_second(2, 27, 42, all_ops, W2)
    acc2[1] = conv_second(3, 14, 42, all_ops, W2)
    loads[4].wait()
    halo.receive_relayed()

    fill_first(0, "rims", zb, *rims, gain1, S, R)
    build_first(0, S, B1, E1)
    for o in (3, 2, 1, 0):
        if o == 3:
            hidden = acc1[1] + conv_first(3, 0, 1, B1, E1, W1)
        elif o == 2:
            hidden = acc1[0] + conv_first(2, 0, 2, B1, E1, W1)
        else:
            hidden = conv_first(o, 0, 3, B1, E1, W1)
        put_second(o, hidden, gain2, keep, Ta, Tb)
        build_second(o, Ta, Tb, *ops)
        build_pair(o, Tb, P2f, P2fe)
        if o == 3:
            merged = acc2[1] + conv_second(3, 0, 14, all_ops, W2)
        elif o == 2:
            merged = acc2[0] + conv_second(2, 0, 27, all_ops, W2)
        else:
            merged = conv_second(o, 0, 42, all_ops, W2)
        put_merged(o, merged, keep, Mg)
    downscale(Mg, W3, Q, out)
    halo.finish()


VM = pl.BlockSpec(memory_space=pltpu.VMEM)
HBM = pl.BlockSpec(memory_space=pltpu.HBM)
LANDING = [(4, 8, 1536), (8, 8, 1536), (8, 8, 256), (8, 8, 384), (8, 8, 256), (8, 8, 384)]


def field(x, g1, g2, k1, k2, sc, k3):
    bf, f32, dma = jnp.bfloat16, jnp.float32, pltpu.SemaphoreType.DMA
    shapes = [
        ((4, 8, 1536), bf), ((1, 96), f32), ((1, 192), f32),
        (((8 * 13 + 8) * 32, 128), f32), (((4 * 9 + 8) * 32, 128), f32),
        ((3, 8, 13, 16, 128), bf), ((3, 7, 8, 16, 128), bf),
        (((6 * 11 + 8) * 32, 128), f32), (((6 * 11 + 8) * 32, 128), f32),
        ((3, 6, 11, 16, 128), bf), ((6, 11, 16, 128), bf), ((6, 9, 16, 128), bf), ((6, 9, 16, 128), bf),
        ((3, 3, 6, 16, 128), bf), ((3, 6, 16, 128), bf), ((6, 16, 128), bf), ((6, 16, 128), bf),
        ((4, 9, 16, 128), bf), ((4, 16, 128), bf),
        ((27, 128, 192), bf), ((42, 128, 192), bf), ((9, 256, 192), bf),
        ((2, 4 * 9 * 32, 128), f32), ((2, 128, 128), f32), ((2, 224, 192), f32), ((2, 160, 192), f32),
    ]
    return pl.pallas_call(
        field_kernel,
        out_shape=[jax.ShapeDtypeStruct((4, 4, 1536), bf)] + [jax.ShapeDtypeStruct(s, bf) for s in LANDING],
        in_specs=[HBM] * 7,
        out_specs=[VM] * 7,
        scratch_shapes=[pltpu.VMEM(*s) for s in shapes]
        + [dma((5,)), dma((31,)), dma, dma, dma((2, 8)), dma((2, 8)), pltpu.SemaphoreType.REGULAR],
        compiler_params=pltpu.CompilerParams(
            collective_id=0, has_side_effects=True, vmem_limit_bytes=40 * 2**20),
    )(x, g1, g2, k1, k2, sc, k3)[0]


def local(x, g1, g2, k1, k2, sc, dw):
    keep = [pltpu.with_memory_space_constraint(a, pltpu.HBM) for a in (x, g1.reshape(1, 96), g2.reshape(1, 192), k1.reshape(27, 96, 192), k2.reshape(27, 192, 192), sc, dw.reshape(9, 192, 192))]
    return field(*keep)


def solution(mesh):
    placed = (P("tm", "height", "width"), P(), P(), P(), P(), P(), P())
    return jax.shard_map(
        local, mesh=mesh, in_specs=placed, out_specs=P("tm", "height", "width"), check_vma=False
    )
```

```python
import functools

import jax
import jax.numpy as jnp
from jax import lax
from jax.experimental import pallas as pl
from jax.experimental.pallas import tpu as pltpu
from jax.sharding import PartitionSpec as P

MESH = pl.DeviceIdType.MESH
epsilon = 1e-06
SIDES = [(-1, 0), (1, 0), (0, -1), (0, 1), (-1, -1), (-1, 1), (1, -1), (1, 1)]

BATCH = [(4, 4), (2, 2), (0, 2)]


class Halo:
    def __init__(self, x, zb, rb, cl, cr, kl, kr, zs, zr, ss, sr, credit):
        self.x, self.zb, self.rb, self.cl, self.cr, self.kl, self.kr = x, zb, rb, cl, cr, kl, kr
        self.zs, self.zr, self.ss, self.sr, self.credit = zs, zr, ss, sr, credit
        self.t, self.h, self.w = (lax.axis_index(a) for a in ("tm", "height", "width"))
        self.nt, self.nh, self.nw = (lax.axis_size(a) for a in ("tm", "height", "width"))

    def exists(self, dh, dw):
        ok = None
        for pos, by, n in ((self.h, dh, self.nh), (self.w, dw, self.nw)):
            if by:
                one = pos > 0 if by < 0 else pos < n - 1
                ok = one if ok is None else jnp.logical_and(ok, one)
        return ok

    def greet(self):
        t, h, w = self.t, self.h, self.w
        bar = pltpu.get_barrier_semaphore()
        for dh, dw in SIDES:
            @pl.when(self.exists(dh, dw))
            def _():
                pl.semaphore_signal(bar, inc=1, device_id=(t, h + dh, w + dw), device_id_type=MESH)

        @pl.when(t < self.nt - 1)
        def _():
            pl.semaphore_signal(bar, inc=1, device_id=(t + 1, h, w), device_id_type=MESH)

    def clear_outside(self):
        def clear(ref, rows, n):
            ref[:, pl.ds(rows, n), :] = jnp.zeros((8, n, ref.shape[2]), ref.dtype)

        @pl.when(self.t == 0)
        def _():
            self.zb[...] = jnp.zeros_like(self.zb)
            for ref in (self.rb, self.cl, self.cr, self.kl, self.kr):
                ref[pl.ds(0, 4)] = jnp.zeros((4,) + ref.shape[1:], ref.dtype)

        @pl.when(self.h == 0)
        def _():
            for ref in (self.rb, self.kl, self.kr):
                clear(ref, 6, 2)

        @pl.when(self.h == self.nh - 1)
        def _():
            for ref in (self.rb, self.kl, self.kr):
                clear(ref, 0, 4)

        @pl.when(self.w == 0)
        def _():
            clear(self.cl, 0, 8)
            clear(self.kl, 0, 8)

        @pl.when(self.w == self.nw - 1)
        def _():
            clear(self.cr, 0, 8)
            clear(self.kr, 0, 8)

    def meet(self):
        count = (self.t > 0).astype(jnp.int32)
        for side in SIDES:
            count += self.exists(*side).astype(jnp.int32)
        pl.semaphore_wait(pltpu.get_barrier_semaphore(), count)

        @pl.when(self.t > 0)
        def _():
            pl.semaphore_signal(
                self.credit, inc=1, device_id=(self.t - 1, self.h, self.w), device_id_type=MESH)

    def along(self, batch):
        frames = pl.ds(BATCH[batch][0], 2)
        return pltpu.make_async_remote_copy(
            src_ref=self.x.at[frames], dst_ref=self.zb.at[frames],
            send_sem=self.zs.at[batch], recv_sem=self.zr.at[batch],
            device_id=(self.t + 1, self.h, self.w), device_id_type=MESH)

    def across(self, i, batch):
        dh, dw = SIDES[i]
        rows = {-1: pl.ds(0, 4), 0: pl.ds(0, 8), 1: pl.ds(6, 2)}[dh]
        lanes = {-1: pl.ds(0, 384), 0: pl.ds(0, 1536), 1: pl.ds(1280, 256)}[dw]
        if dw == 0:
            dst = self.rb
        elif dh == 0:
            dst = self.cl if dw == 1 else self.cr
        else:
            dst = self.kl if dw == 1 else self.kr
        first, n = BATCH[batch]
        src = self.zb.at[pl.ds(first, n), rows, lanes] if batch else self.x.at[:, rows, lanes]
        return pltpu.make_async_remote_copy(
            src_ref=src, dst_ref=dst.at[pl.ds(first, n), rows],
            send_sem=self.ss.at[batch, i], recv_sem=self.sr.at[batch, i],
            device_id=(self.t, self.h + dh, self.w + dw), device_id_type=MESH)

    def send_across(self, batch):
        for i, side in enumerate(SIDES):
            @pl.when(self.exists(*side))
            def _():
                self.across(i, batch).start()

    def receive_across(self, batch):
        for i, (dh, dw) in enumerate(SIDES):
            @pl.when(self.exists(-dh, -dw))
            def _():
                self.across(i, batch).wait_recv()

    def sent_across(self, batch):
        for i, side in enumerate(SIDES):
            @pl.when(self.exists(*side))
            def _():
                self.across(i, batch).wait_send()

    def send_along(self):
        @pl.when(self.t < self.nt - 1)
        def _():
            pl.semaphore_wait(self.credit, 1)
            self.along(1).start()
            self.along(2).start()

    def relay(self, batch):
        @pl.when(self.t > 0)
        def _():
            self.along(batch).wait_recv()
            self.send_across(batch)

    def receive_relayed(self, batch):
        @pl.when(self.t > 0)
        def _():
            self.receive_across(batch)

    def finish(self):
        self.sent_across(0)

        @pl.when(self.t > 0)
        def _():
            self.sent_across(1)
            self.sent_across(2)

        @pl.when(self.t < self.nt - 1)
        def _():
            self.along(1).wait_send()
            self.along(2).wait_send()


def activate(v, gain, n):
    meansq = jnp.sum(v * v, axis=-1, keepdims=True) * (1.0 / n)
    half = v * lax.rsqrt(meansq + epsilon) * (0.5 * gain)
    return half + half * jnp.tanh(half)


def take_column(ref, first, n, begin):
    tile, off = divmod(begin, 128)
    lane = lax.broadcasted_iota(jnp.int32, (8 * n, 128), 1)

    def lanes(k):
        v = ref[pl.ds(first, n), :, pl.ds(128 * k, 128)].astype(jnp.float32).reshape(8 * n, 128)
        return pltpu.roll(v, 128 - off, 1) if off else v

    v = lanes(tile)
    if off + 96 > 128:
        v = jnp.where(lane < 128 - off, v, lanes(tile + 1))
    return jnp.where(lane < 96, v, 0.0)


def at(frame, row, col, rows):
    return (frame * rows + row) * 32 + 8 + col


def fill_first(f0, n, part, blk, rb, cl, cr, kl, kr, gain, S, R):
    def put(v, col, rim):
        a = activate(v, gain, 96)
        for k in range(n):
            e = f0 + k
            piece = a[8 * k : 8 * k + 8]
            raw = v[8 * k : 8 * k + 8]
            if rim:
                S[pl.ds(at(e, 10, col, 13), 3, stride=32), :] = piece[0:3]
                S[pl.ds(at(e, 0, col, 13), 2, stride=32), :] = piece[6:8]
            else:
                S[pl.ds(at(e, 2, col, 13), 8, stride=32), :] = piece
            if e >= 4 and 0 <= col <= 16:
                if rim:
                    R[pl.ds(at(e - 4, 8, col, 9), 1), :] = raw[0:1]
                else:
                    R[pl.ds(at(e - 4, 0, col, 9), 8, stride=32), :] = raw

    if part == "block":
        for c in range(16):
            put(take_column(blk, 0, n, 96 * c), c, False)
        return
    for c in range(16):
        put(take_column(rb, f0, n, 96 * c), c, True)
    for c in (-2, -1):
        put(take_column(cl, f0, n, 64 + 96 * (c + 2)), c, False)
        put(take_column(kl, f0, n, 64 + 96 * (c + 2)), c, True)
    for c in (16, 17, 18):
        put(take_column(cr, f0, n, 96 * (c - 16)), c, False)
        put(take_column(kr, f0, n, 96 * (c - 16)), c, True)


def build_first(f0, n, S, B1, E1):
    for e in range(f0, f0 + n):
        for r in range(13):
            for dc in range(3):
                B1[dc, e, r] = S[pl.ds(at(e, r, dc - 1, 13), 16), :].astype(jnp.bfloat16)
        for dr in range(3):
            for k, c in enumerate((-2, -1, 0, 15, 16, 17, 18)):
                E1[dr, k, e] = S[pl.ds(at(e, dr, c, 13), 16, stride=32), :].astype(jnp.bfloat16)


TAPS = [(dr, dc) for dr in range(3) for dc in range(3)]


class Keep:
    def __init__(self, h, w, nh, nw):
        f32 = jnp.float32
        self.top, self.bottom = (h > 0).astype(f32), (h < nh - 1).astype(f32)
        self.left, self.right = (w > 0).astype(f32), (w < nw - 1).astype(f32)

    def rows(self, first_below, top):
        row = lax.broadcasted_iota(jnp.int32, (16, 128), 0)
        m = jnp.where(row >= first_below, self.bottom, 1.0)
        return jnp.where(row == 0, self.top, m) if top else m


def conv_first(o, lo, hi, B1, E1, W1):
    rows = [
        jnp.concatenate(
            [B1[dc, o + dt, pl.ds(dr, 11)].reshape(176, 128)] + [E1[dr, k + dc, o + dt] for k in (0, 3, 4)], axis=0)
        for dt in range(lo, hi) for dr, dc in TAPS
    ]
    w = W1[pl.ds(9 * lo, 9 * (hi - lo))].reshape((hi - lo) * 9 * 128, 192)
    return jnp.dot(jnp.concatenate(rows, axis=1), w, preferred_element_type=jnp.float32)


def put_second(f, hidden, gain, keep, Ta, Tb):
    second = activate(hidden, gain, 192)
    pa = second[:, 0:128]
    pb = jnp.concatenate([second[:, 128:192], second[:, 128:192]], axis=1)
    for r in range(11):
        for T, p in ((Ta, pa), (Tb, pb)):
            v = p[16 * r : 16 * r + 16]
            if r == 0:
                v = v * keep.top
            if r >= 9:
                v = v * keep.bottom
            T[pl.ds(at(f, r, 0, 11), 16), :] = v
    inside = keep.rows(9, True)
    for k, c in enumerate((-1, 16, 17)):
        m = 176 + 16 * k
        side = inside * (keep.left if k == 0 else keep.right)
        for T, p in ((Ta, pa), (Tb, pb)):
            T[pl.ds(at(f, 0, c, 11), 11, stride=32), :] = (p[m : m + 16] * side)[0:11]


def halves(a, b):
    lane = lax.broadcasted_iota(jnp.int32, a.shape, 1)
    return jnp.where(lane < 64, a, b).astype(jnp.bfloat16)


def build_second(f, Ta, Tb, A2, P01, P2r, D2, A2e, P01e, P2re, D2e):
    for r in range(11):
        spans = [pl.ds(at(f, r, dc - 1, 11), 16) for dc in range(3)]
        for dc in range(3):
            A2[dc, f, r] = Ta[spans[dc], :].astype(jnp.bfloat16)
        P01[f, r] = halves(Tb[spans[0], :], Tb[spans[1], :])
        if r < 9:
            P2r[f, r] = halves(Tb[spans[2], :], Tb[pl.ds(at(f, r + 1, 1, 11), 16), :])
        if r >= 2:
            D2[f, r - 2] = Tb[spans[2], :].astype(jnp.bfloat16)
    for dr in range(3):
        spans = [pl.ds(at(f, dr, c, 11), 16, stride=32) for c in (15, 16, 17)]
        for k in range(3):
            A2e[dr, k, f] = Ta[spans[k], :].astype(jnp.bfloat16)
        P01e[dr, f] = halves(Tb[spans[0], :], Tb[spans[1], :])
    rows = [Tb[pl.ds(at(f, dr, 17, 11), 16, stride=32), :] for dr in range(3)]
    P2re[f] = halves(rows[0], rows[1])
    D2e[f] = rows[2].astype(jnp.bfloat16)


def build_pair(f, Tb, P2f, P2fe):
    for r in range(2, 11):
        P2f[f, r - 2] = halves(Tb[pl.ds(at(f, r, 1, 11), 16), :], Tb[pl.ds(at(f + 1, r, 1, 11), 16), :])
    P2fe[f] = halves(*(Tb[pl.ds(at(g, 2, 17, 11), 16, stride=32), :] for g in (f, f + 1)))


BASE = (0, 14, 27)


def tile_of(dt, dr, dc):
    if dc < 2:
        return BASE[dt] + 9 + dr, dc
    if dr < 2:
        return BASE[dt] + 12, dr
    return (13, dt) if dt < 2 else (40, 0)


def conv_second(f, first, last, ops, W2):
    A2, P01, P2r, D2, A2e, P01e, P2re, D2e, P2f, P2fe, R = ops

    def tile(i):
        if i == 41:
            return [R[pl.ds(at(f, r, 0, 9), 16), :].astype(jnp.bfloat16) for r in range(9)] + [
                R[pl.ds(at(f, 0, 16, 9), 16, stride=32), :].astype(jnp.bfloat16)]
        if i == 13:
            return [P2f[f].reshape(144, 128), P2fe[f]]
        if i == 40:
            return [D2[f + 2].reshape(144, 128), D2e[f + 2]]
        dt = 2 if i >= BASE[2] else 1 if i >= BASE[1] else 0
        k, g = i - BASE[dt], f + dt
        if k < 9:
            dr, dc = TAPS[k]
            return [A2[dc, g, pl.ds(dr, 9)].reshape(144, 128), A2e[dr, dc, g]]
        if k < 12:
            return [P01[g, pl.ds(k - 9, 9)].reshape(144, 128), P01e[k - 9, g]]
        return [P2r[g].reshape(144, 128), P2re[g]]

    lhs = jnp.concatenate([jnp.concatenate(tile(i), axis=0) for i in range(first, last)], axis=1)
    w = W2[pl.ds(first, last - first)].reshape((last - first) * 128, 192)
    return jnp.dot(lhs, w, preferred_element_type=jnp.float32)


def put_merged(f, merged, keep, Mg):
    merged = merged.astype(jnp.bfloat16).astype(jnp.float32)
    pb = jnp.concatenate([merged[:, 128:192], jnp.zeros((160, 64), jnp.float32)], axis=1)
    side = keep.rows(8, False) * keep.right
    for p, v in enumerate((merged[:, 0:128], pb)):
        for r in range(9):
            part = v[16 * r : 16 * r + 16]
            Mg[p, pl.ds((f * 9 + r) * 32, 16), :] = part * keep.bottom if r == 8 else part
        Mg[p, pl.ds(f * 288 + 16, 9, stride=32), :] = (v[144:160] * side)[0:9]


def downscale(f0, n, Mg, W3, Q, out_ref):
    cols = []
    for dr in range(3):
        for dc in range(3):
            for p in range(2):
                cols.append(jnp.concatenate(
                    [Mg[p, pl.ds((f * 9 + 2 * i + dr) * 32 + dc, 8, stride=2), :]
                     for f in range(f0, f0 + n) for i in range(4)], axis=0).astype(jnp.bfloat16))
    res = jnp.dot(
        jnp.concatenate(cols, axis=1), W3[...].reshape(9 * 256, 192), preferred_element_type=jnp.float32
    )
    Q[0, pl.ds(32 * f0, 32 * n)] = res[:, 0:128]
    Q[1, pl.ds(32 * f0, 32 * n), 0:64] = res[:, 128:192]
    for f in range(f0, f0 + n):
        for j in range(8):
            s = pl.ds(f * 32 + j, 4, stride=8)
            out_ref[f, :, 192 * j : 192 * j + 192] = jnp.concatenate(
                [Q[0, s, :], Q[1, s, :][:, 0:64]], axis=1
            ).astype(jnp.bfloat16)


def field_kernel(x, g1, g2, k1, k2, sc, k3, out,
                 zb, rb, cl, cr, kl, kr, xs, ga, gb, S, R, B1, E1, Ta, Tb, A2, P01, P2r, D2, A2e, P01e, P2re, D2e, P2f, P2fe,
                 W1, W2, W3, Mg, Q, acc1, acc2, sem, wsem, zs, zr, ss, sr, credit):
    halo = Halo(x, zb, rb, cl, cr, kl, kr, zs, zr, ss, sr, credit)
    rims = (rb, cl, cr, kl, kr)
    halo.greet()
    loads = [
        pltpu.make_async_copy(x, xs, sem.at[0]),
        pltpu.make_async_copy(g1, ga, sem.at[1]),
        pltpu.make_async_copy(g2, gb, sem.at[2]),
        pltpu.make_async_copy(k1, W1.at[:, pl.ds(0, 96), :], sem.at[3]),
        pltpu.make_async_copy(k3, W3.at[:, pl.ds(0, 192), :], sem.at[4]),
    ]
    loads2 = [pltpu.make_async_copy(sc, W2.at[41, pl.ds(0, 96), :], wsem.at[30])]
    for dt in range(3):
        loads2.append(pltpu.make_async_copy(
            k2.at[pl.ds(9 * dt, 9), pl.ds(0, 128), :], W2.at[pl.ds(BASE[dt], 9)], wsem.at[27 + dt]))
        for n, (dr, dc) in enumerate(TAPS):
            i, half = tile_of(dt, dr, dc)
            loads2.append(pltpu.make_async_copy(
                k2.at[9 * dt + n, pl.ds(128, 64), :], W2.at[i, pl.ds(64 * half, 64), :], wsem.at[9 * dt + n]))
    for c in loads:
        c.start()
    halo.clear_outside()
    halo.meet()
    halo.send_across(0)
    for c in loads2:
        c.start()
    W1[:, 96:128, :] = jnp.zeros((27, 32, 192), jnp.bfloat16)
    W2[40, 64:128, :] = jnp.zeros((64, 192), jnp.bfloat16)
    W2[41, 96:128, :] = jnp.zeros((32, 192), jnp.bfloat16)
    W3[:, 192:256, :] = jnp.zeros((9, 64, 192), jnp.bfloat16)
    Mg[1] = jnp.zeros(Mg.shape[1:], jnp.float32)
    for c in loads[:3]:
        c.wait()
    gain1 = jnp.concatenate([ga[...], jnp.zeros((1, 32), jnp.float32)], axis=1)
    gain2 = gb[...]
    keep = Keep(halo.h, halo.w, halo.nh, halo.nw)
    ops = (A2, P01, P2r, D2, A2e, P01e, P2re, D2e)
    all_ops = ops + (P2f, P2fe, R)

    fill_first(4, 4, "block", xs, *rims, gain1, S, R)
    halo.send_along()
    halo.relay(1)
    halo.relay(2)
    halo.receive_across(0)
    loads[3].wait()
    fill_first(4, 4, "rims", xs, *rims, gain1, S, R)
    build_first(4, 4, S, B1, E1)
    for o in (4, 5):
        put_second(o, conv_first(o, 0, 3, B1, E1, W1), gain2, keep, Ta, Tb)
    fill_first(0, 4, "block", zb, *rims, gain1, S, R)
    acc1[0] = conv_first(2, 2, 3, B1, E1, W1)
    acc1[1] = conv_first(3, 1, 3, B1, E1, W1)
    for o in (4, 5):
        build_second(o, Ta, Tb, *ops)
    for c in loads2:
        c.wait()
    halo.receive_relayed(1)

    fill_first(2, 2, "rims", zb, *rims, gain1, S, R)
    build_first(2, 2, S, B1, E1)
    acc2[3] = conv_second(3, 14, 42, all_ops, W2)
    acc2[2] = conv_second(2, 27, 42, all_ops, W2)
    for o in (3, 2):
        put_second(o, acc1[o - 2] + conv_first(o, 0, 4 - o, B1, E1, W1), gain2, keep, Ta, Tb)
        build_second(o, Ta, Tb, *ops)
        build_pair(o, Tb, P2f, P2fe)
    loads[4].wait()
    halo.receive_relayed(2)

    fill_first(0, 2, "rims", zb, *rims, gain1, S, R)
    build_first(0, 2, S, B1, E1)
    put_merged(3, acc2[3] + conv_second(3, 0, 14, all_ops, W2), keep, Mg)
    put_merged(2, acc2[2] + conv_second(2, 0, 27, all_ops, W2), keep, Mg)
    put_second(1, conv_first(1, 0, 3, B1, E1, W1), gain2, keep, Ta, Tb)
    acc2[1] = conv_second(1, 14, 42, all_ops, W2)
    build_second(1, Ta, Tb, *ops)
    build_pair(1, Tb, P2f, P2fe)
    put_second(0, conv_first(0, 0, 3, B1, E1, W1), gain2, keep, Ta, Tb)
    acc2[0] = conv_second(0, 14, 42, all_ops, W2)
    downscale(2, 2, Mg, W3, Q, out)
    put_merged(1, acc2[1] + conv_second(1, 0, 14, all_ops, W2), keep, Mg)
    build_second(0, Ta, Tb, *ops)
    build_pair(0, Tb, P2f, P2fe)
    put_merged(0, acc2[0] + conv_second(0, 0, 14, all_ops, W2), keep, Mg)
    downscale(0, 2, Mg, W3, Q, out)
    halo.finish()


VM = pl.BlockSpec(memory_space=pltpu.VMEM)
HBM = pl.BlockSpec(memory_space=pltpu.HBM)
LANDING = [(4, 8, 1536), (8, 8, 1536), (8, 8, 256), (8, 8, 384), (8, 8, 256), (8, 8, 384)]


def field(x, g1, g2, k1, k2, sc, k3):
    bf, f32, dma = jnp.bfloat16, jnp.float32, pltpu.SemaphoreType.DMA
    shapes = [
        ((4, 8, 1536), bf), ((1, 96), f32), ((1, 192), f32),
        (((8 * 13 + 8) * 32, 128), f32), (((4 * 9 + 8) * 32, 128), f32),
        ((3, 8, 13, 16, 128), bf), ((3, 7, 8, 16, 128), bf),
        (((6 * 11 + 8) * 32, 128), f32), (((6 * 11 + 8) * 32, 128), f32),
        ((3, 6, 11, 16, 128), bf), ((6, 11, 16, 128), bf), ((6, 9, 16, 128), bf), ((6, 9, 16, 128), bf),
        ((3, 3, 6, 16, 128), bf), ((3, 6, 16, 128), bf), ((6, 16, 128), bf), ((6, 16, 128), bf),
        ((4, 9, 16, 128), bf), ((4, 16, 128), bf),
        ((27, 128, 192), bf), ((42, 128, 192), bf), ((9, 256, 192), bf),
        ((2, 44 * 32, 128), f32), ((2, 192, 128), f32), ((2, 224, 192), f32), ((4, 160, 192), f32),
    ]
    return pl.pallas_call(
        field_kernel,
        out_shape=jax.ShapeDtypeStruct((4, 4, 1536), bf),
        in_specs=[HBM] * 7,
        out_specs=VM,
        scratch_shapes=[pltpu.VMEM(s, bf) for s in LANDING] + [pltpu.VMEM(*s) for s in shapes]
        + [dma((5,)), dma((31,)), dma((3,)), dma((3,)), dma((3, 8)), dma((3, 8)), pltpu.SemaphoreType.REGULAR],
        compiler_params=pltpu.CompilerParams(
            collective_id=0, has_side_effects=True, vmem_limit_bytes=40 * 2**20),
    )(x, g1, g2, k1, k2, sc, k3)


def local(x, g1, g2, k1, k2, sc, dw):
    keep = [pltpu.with_memory_space_constraint(a, pltpu.HBM) for a in (x, g1.reshape(1, 96), g2.reshape(1, 192), k1.reshape(27, 96, 192), k2.reshape(27, 192, 192), sc, dw.reshape(9, 192, 192))]
    return field(*keep)


def solution(mesh):
    placed = (P("tm", "height", "width"), P(), P(), P(), P(), P(), P())
    return jax.shard_map(
        local, mesh=mesh, in_specs=placed, out_specs=P("tm", "height", "width"), check_vma=False
    )
```
